32 devices in a mesh: clip: 2 (over x), space: 4 (over y, core), tm: 4 (over z).
Axes of the slice: x: 2, y: 2, z: 4, core: 2. Of those that a mesh axis runs over, the one named last changes fastest.
Arguments:
- block_input: bfloat16 [8, 12, 160, 384], P(('clip', 'tm'), 'space'), parts along dimension 0, may hold values from -24 to 24, as said below
- conv_input: bfloat16 [8, 12, 160, 384], P(('clip', 'tm'), 'space'), parts along dimension 0, may hold values from -24 to 24, as said below
- norm_gain: float32 [384], replicated, may hold values from 0.1 to 1.9
- norm_bias: float32 [384], replicated, may hold values from -3 to 3
- conv_weight: bfloat16 [3, 3, 3, 384, 384], replicated, may hold values from -0.0625 to 0.0625
- conv_bias: float32 [384], replicated, may hold values from -1.5 to 1.5
- attn_gain: float32 [384], replicated, may hold values from 0.1 to 1.9
- attn_bias: float32 [384], replicated, may hold values from -1.5 to 1.5
- query_weight: bfloat16 [384, 384], replicated, may hold values from -4 to 4
- query_bias: float32 [384], replicated, may hold values from -1.5 to 1.5
- key_weight: bfloat16 [384, 384], replicated, may hold values from -4 to 4
- value_weight: bfloat16 [384, 384], replicated, may hold values from -0.3125 to 0.3125
- value_bias: float32 [384], replicated, may hold values from -3 to 3
- out_weight: bfloat16 [384, 384], replicated, may hold values from -0.3125 to 0.3125
- out_bias: float32 [384], replicated, may hold values from -3 to 3
Outputs:
- block_output: bfloat16 [8, 12, 160, 384], P(('clip', 'tm'), 'space'), parts along dimension 0
The draws below stay inside these ranges and needn't reach their ends.
There are 2 independent parts, one for each index of `clip`. The reference program is written for one: setup_inputs(seed, part) draws one part's arguments, and reference() takes and returns one part's arrays. A program takes and returns all parts, laid end to end along the dimension named above; an argument that names none is the same for every part. Nothing has to cross between parts.
Inputs may be any that keep to these rules, and one draw needn't show every extreme that they name: `block_input`: finite activations. `conv_input`: finite activations.
All inputs are finite; a program needn't handle non-finite values.
Results may differ from the reference program's by a relative error of at most 0.0075.
Values may be sent and summed in bfloat16 or wider, within the bound.
No kernel may reach another device: no remote copies, remote signals or barrier semaphores. Data moves between devices by JAX's collectives and lax.ppermute only.
A program may use at most 128 MiB of HBM per device.

```python
import jax
import jax.numpy as jnp
from jax import lax

C = 384
WIDTH = 160
ROWS = 12
FRAMES = 4


def activation_draw(key, salt):
    base_key = jax.random.fold_in(key, salt)
    first_key, second_key = jax.random.split(base_key)
    shape = (FRAMES, ROWS, WIDTH, C)
    base = jax.random.truncated_normal(first_key, -4.0, 4.0, shape, jnp.float32)
    row_pos = jnp.arange(ROWS, dtype=jnp.float32) / (ROWS - 1)
    row_scale = 0.3 * jnp.exp(jnp.log(10.0) * row_pos)
    chan_scale = jnp.exp(jax.random.uniform(second_key, (C,), jnp.float32, -0.55, 0.55))
    return base * row_scale[None, :, None, None] * chan_scale


def projection_draw(key, salt):
    base_key = jax.random.fold_in(key, salt)
    noise = jax.random.truncated_normal(base_key, -4.0, 4.0, (C, C), jnp.float32)
    return 2.0 * noise * C ** (-0.5)


def draw_block_input(key, part):
    return activation_draw(key, 11).astype(jnp.bfloat16)


def draw_conv_input(key, part):
    return activation_draw(key, 23).astype(jnp.bfloat16)


def draw_query_weight(key, part):
    return projection_draw(key, 37).astype(jnp.bfloat16)


def draw_key_weight(key, part):
    return projection_draw(key, 41).astype(jnp.bfloat16)


def bell_draw(own_key, dims, width, limit, held_as=jnp.bfloat16):
    entries = jax.random.normal(own_key, dims, jnp.float32) * width
    return jnp.minimum(jnp.maximum(entries, -limit), limit).astype(held_as)


def setup_inputs(seed: int = 0, part: int = 0) -> dict:
    arg_keys = jax.random.split(jax.random.key(seed), 16)
    own_keys = jax.random.split(jax.random.fold_in(arg_keys[15], part), 16)
    block_input = draw_block_input(jax.random.fold_in(jax.random.fold_in(arg_keys[15], part), 71), part)
    conv_input = draw_conv_input(jax.random.fold_in(jax.random.fold_in(arg_keys[15], part), 71), part)
    norm_gain = jnp.clip(1.0 + 0.18 * jax.random.normal(arg_keys[2], (C,), jnp.float32), 0.1, 1.9)
    norm_bias = bell_draw(arg_keys[3], (C,), 0.5, 3.0, jnp.float32)
    conv_weight = bell_draw(arg_keys[4], (3, 3, 3, C, C), (27 * C) ** -0.5, 0.0625)
    conv_bias = bell_draw(arg_keys[5], (C,), 0.25, 1.5, jnp.float32)
    attn_gain = jnp.clip(1.0 + 0.18 * jax.random.normal(arg_keys[6], (C,), jnp.float32), 0.1, 1.9)
    attn_bias = bell_draw(arg_keys[7], (C,), 0.25, 1.5, jnp.float32)
    query_weight = draw_query_weight(jax.random.fold_in(arg_keys[15], 71), part)
    query_bias = bell_draw(arg_keys[9], (C,), 0.25, 1.5, jnp.float32)
    key_weight = draw_key_weight(jax.random.fold_in(arg_keys[15], 71), part)
    value_weight = bell_draw(arg_keys[11], (C, C), C ** -0.5, 0.3125)
    value_bias = bell_draw(arg_keys[12], (C,), 0.5, 3.0, jnp.float32)
    out_weight = bell_draw(arg_keys[13], (C, C), C ** -0.5, 0.3125)
    out_bias = bell_draw(arg_keys[14], (C,), 0.5, 3.0, jnp.float32)
    return dict(block_input=block_input, conv_input=conv_input, norm_gain=norm_gain, norm_bias=norm_bias, conv_weight=conv_weight, conv_bias=conv_bias, attn_gain=attn_gain, attn_bias=attn_bias, query_weight=query_weight, query_bias=query_bias, key_weight=key_weight, value_weight=value_weight, value_bias=value_bias, out_weight=out_weight, out_bias=out_bias)


def rms_norm(field, gain, bias):
    mean_square = lax.optimization_barrier(jnp.mean(field * field, axis=-1, keepdims=True))
    return field * lax.rsqrt(mean_square + 1e-06) * gain + bias

def causal_conv(padded, conv_weight, frame_count, row_count, columns):
    channels = padded.shape[-1]
    running = jnp.zeros((frame_count * row_count * columns, channels), jnp.float32)
    for tap_t in range(3):
        for tap_y in range(3):
            window = padded[tap_t:tap_t + frame_count, tap_y:tap_y + row_count]
            joined = jnp.concatenate([window[:, :, tap_x:tap_x + columns] for tap_x in range(3)], axis=-1)
            joined = joined.reshape(-1, 3 * channels)
            kernel = conv_weight[tap_t, tap_y].reshape(3 * channels, channels)
            running = running + jnp.dot(joined, kernel, preferred_element_type=jnp.float32)
    return running.reshape(frame_count, row_count, columns, channels)

def reference(block_input, conv_input, norm_gain, norm_bias, conv_weight, conv_bias, attn_gain, attn_bias, query_weight, query_bias, key_weight, value_weight, value_bias, out_weight, out_bias):
    field = conv_input.astype(jnp.float32)
    activated = jax.nn.silu(rms_norm(field, norm_gain, norm_bias)).astype(jnp.bfloat16)
    padded = jnp.pad(activated, ((2, 0), (1, 1), (1, 1), (0, 0)))
    convolved = causal_conv(padded, conv_weight, FRAMES, ROWS, WIDTH) + conv_bias
    mixed = (block_input.astype(jnp.float32) + convolved).astype(jnp.bfloat16)
    mixed_wide = mixed.astype(jnp.float32)
    normed = rms_norm(mixed_wide, attn_gain, attn_bias).astype(jnp.bfloat16)
    flat_rows = normed.reshape(FRAMES, ROWS * WIDTH, C)
    score_scale = C ** (-0.5)

    def one_frame(frame_rows):
        queries = (jnp.dot(frame_rows, query_weight, preferred_element_type=jnp.float32) + query_bias).astype(jnp.bfloat16)
        key_rows = jnp.dot(frame_rows, key_weight, preferred_element_type=jnp.float32).astype(jnp.bfloat16)
        value_rows = (jnp.dot(frame_rows, value_weight, preferred_element_type=jnp.float32) + value_bias).astype(jnp.bfloat16)
        scores = jnp.dot(queries, key_rows.T, preferred_element_type=jnp.float32) * score_scale
        highest = lax.optimization_barrier(jnp.max(scores, axis=-1, keepdims=True))
        expd = jnp.exp(scores - highest)
        weights = expd.astype(jnp.bfloat16)
        numer = jnp.dot(weights, value_rows, preferred_element_type=jnp.float32)
        return (numer / lax.optimization_barrier(jnp.sum(expd, axis=-1, keepdims=True))).astype(jnp.bfloat16)
    attended = lax.map(one_frame, flat_rows)
    projected = jnp.dot(attended.reshape(-1, C), out_weight, preferred_element_type=jnp.float32) + out_bias
    return (mixed_wide + projected.reshape(mixed_wide.shape)).astype(jnp.bfloat16)
```

```python
import functools

import jax
import jax.numpy as jnp
from jax import lax
from jax.experimental import pallas as pl
from jax.experimental.pallas import tpu as pltpu
from jax.sharding import PartitionSpec as P

LOG2_E = 1.4426950408889634
VMEM = pltpu.VMEM


def ring(count, step):
    return [(i, (i + step) % count) for i in range(count)]


def pairs(count):
    return [(i, i ^ 1) for i in range(count)]


def edges_of(field):
    bands = lax.axis_size("space")
    rows = field.shape[1]
    above = lax.ppermute(field[:, rows - 1 :], "space", ring(bands, 1))
    below = lax.ppermute(field[:, :1], "space", ring(bands, -1))
    return above, below


def rms_scaled(wide, gain, bias):
    mean_square = jnp.mean(wide * wide, axis=-1, keepdims=True)
    return wide * lax.rsqrt(mean_square + 1e-06) * gain + bias


def fill_row(taps, at, cells, keep, gain, bias):
    columns, channels = cells.shape
    wide = rms_scaled(cells.astype(jnp.float32), gain, bias)
    active = wide / (1.0 + jnp.exp(-wide))
    column = lax.broadcasted_iota(jnp.int32, (columns, channels), 0)
    if keep is not None:
        active = jnp.where(keep, active, 0.0)
    left = jnp.where(column == 0, 0.0, pltpu.roll(active, 1, 0))
    right = jnp.where(column == columns - 1, 0.0, pltpu.roll(active, columns - 1, 0))
    span = pl.ds(at * columns, columns)
    taps[span, 0:channels] = left.astype(jnp.bfloat16)
    taps[span, channels : 2 * channels] = active.astype(jnp.bfloat16)
    taps[span, 2 * channels : 3 * channels] = right.astype(jnp.bfloat16)


def conv_body(first, last, columns, *refs):
    (flags, field, above, below, gain, bias, kernel, start), refs = refs[:8], refs[8:]
    if first:
        conv_bias, total, taps = refs
    elif last:
        attn_gain, attn_bias, query_w, query_b, key_w, mixed, normed, queries, taps, total = refs
    else:
        total, taps = refs
    tap = pl.program_id(0)
    cells = field.shape[0]
    rows = cells // columns

    @pl.when(tap == 0)
    def _():
        here, over, under = (flags[0, i] > 0 for i in range(3))
        for row in range(rows):
            fill_row(taps, row + 1, field[row * columns : (row + 1) * columns], here, gain[...], bias[...])
        fill_row(taps, 0, above[...], over, gain[...], bias[...])
        fill_row(taps, rows + 1, below[...], under, gain[...], bias[...])
        if first:
            total[...] = start[...].astype(jnp.float32) + conv_bias[...]
        else:
            total[...] = start[...]

    window = taps[pl.ds(pl.multiple_of(tap * columns, 16), cells), :]
    total[...] += jnp.dot(window, kernel[...], preferred_element_type=jnp.float32)

    if last:

        @pl.when(tap == 2)
        def _():
            channels = field.shape[1]
            rounded = total[...].astype(jnp.bfloat16)
            mixed[...] = rounded
            norm = rms_scaled(rounded.astype(jnp.float32), attn_gain[...], attn_bias[...])
            norm = norm.astype(jnp.bfloat16)
            normed[...] = norm
            query = jnp.dot(norm, query_w[...], preferred_element_type=jnp.float32) + query_b[...]
            query = query.astype(jnp.bfloat16)
            folded = lax.dot_general(
                query, key_w[...], (((1,), (1,)), ((), ())), preferred_element_type=jnp.float32
            )
            queries[...] = (folded * (LOG2_E * float(channels) ** -0.5)).astype(jnp.bfloat16)


def whole(shape):
    return pl.BlockSpec(shape, lambda i: (0,) * len(shape))


def conv_step(which, flags, field, above, below, gain, bias, kernels, start, extra=()):
    _, rows, columns, channels = field.shape
    cells = rows * columns
    first, last = which == 0, which == 2
    flat = (cells, channels)
    taken = kernels.shape[0] // 3 - 1 - which
    scratch = [pltpu.VMEM(((rows + 2) * columns, 3 * channels), jnp.bfloat16)]
    if last:
        out_shape = [jax.ShapeDtypeStruct(flat, jnp.bfloat16)] * 3
        out_specs = [whole(flat)] * 3
        scratch.append(pltpu.VMEM(flat, jnp.float32))
    else:
        out_shape = jax.ShapeDtypeStruct(flat, jnp.float32)
        out_specs = whole(flat)
    arrays = [field.reshape(flat), above.reshape(columns, channels), below.reshape(columns, channels)]
    arrays += [gain, bias]
    specs = [whole(a.shape) for a in arrays]
    specs.append(pl.BlockSpec((None, 3 * channels, channels), lambda i: (3 * taken + i, 0, 0)))
    tail = [start.reshape(flat), *extra]
    specs += [whole(a.shape) for a in tail]
    return pl.pallas_call(
        functools.partial(conv_body, first, last, columns),
        grid=(3,),
        in_specs=[pl.BlockSpec(memory_space=pltpu.SMEM), *specs],
        out_specs=out_specs,
        out_shape=out_shape,
        scratch_shapes=scratch,
        name=("conv_own", "conv_prev", "conv_last")[which],
    )(flags, *arrays, kernels, *tail)


def attn_body(count, resumed, last, *refs):
    queries, refs = refs[0], refs[1:]
    blocks, refs = refs[:count], refs[count:]
    if resumed:
        (numer_in, denom_in, high_in), refs = refs[:3], refs[3:]
    if last:
        value_w, value_b, out_w, out_b, mixed, result = refs
    else:
        numer_out, denom_out, high_out = refs
    cells, channels = queries.shape
    tile = 160 if cells % 160 == 0 else cells
    for part in range(cells // tile):
        span = slice(part * tile, (part + 1) * tile)
        query = queries[span]
        if resumed:
            numer, denom, high = numer_in[span], denom_in[span, 0:1], high_in[span, 0:1]
        else:
            numer = denom = high = None
        for block in blocks:
            keys = block[...]
            scores = lax.dot_general(
                query, keys, (((1,), (1,)), ((), ())), preferred_element_type=jnp.float32
            )
            top = jnp.max(scores, axis=-1, keepdims=True)
            fresh = top if high is None else jnp.maximum(high, top)
            expd = jnp.exp2(scores - fresh)
            added = jnp.dot(expd.astype(jnp.bfloat16), keys, preferred_element_type=jnp.float32)
            count_up = jnp.sum(expd, axis=-1, keepdims=True)
            if high is None:
                numer, denom = added, count_up
            else:
                decay = jnp.exp2(high - fresh)
                numer, denom = numer * decay + added, denom * decay + count_up
            high = fresh
        if last:
            pooled = (numer / denom).astype(jnp.bfloat16)
            attended = jnp.dot(pooled, value_w[...], preferred_element_type=jnp.float32) + value_b[...]
            attended = attended.astype(jnp.bfloat16)
            projected = jnp.dot(attended, out_w[...], preferred_element_type=jnp.float32) + out_b[...]
            result[span] = (mixed[span].astype(jnp.float32) + projected).astype(jnp.bfloat16)
        else:
            numer_out[span] = numer
            denom_out[span] = jnp.broadcast_to(denom, (tile, 128))
            high_out[span] = jnp.broadcast_to(high, (tile, 128))


def attn_step(name, queries, blocks, state, closing=None):
    cells, channels = queries.shape
    arrays = [queries, *blocks, *(state or ())]
    if closing is not None:
        arrays += closing
        out_shape = jax.ShapeDtypeStruct((cells, channels), jnp.bfloat16)
    else:
        out_shape = [
            jax.ShapeDtypeStruct((cells, channels), jnp.float32),
            jax.ShapeDtypeStruct((cells, 128), jnp.float32),
            jax.ShapeDtypeStruct((cells, 128), jnp.float32),
        ]
    vmem = pl.BlockSpec(memory_space=VMEM)
    return pl.pallas_call(
        functools.partial(attn_body, len(blocks), state is not None, closing is not None),
        in_specs=[vmem] * len(arrays),
        out_specs=vmem if closing is not None else [vmem] * 3,
        out_shape=out_shape,
        name=name,
    )(*arrays)


def single_frame(
    block_input,
    conv_input,
    norm_gain,
    norm_bias,
    conv_weight,
    conv_bias,
    attn_gain,
    attn_bias,
    query_weight,
    query_bias,
    key_weight,
    value_weight,
    value_bias,
    out_weight,
    out_bias,
):
    _, rows, columns, channels = block_input.shape
    bands, groups = lax.axis_size("space"), lax.axis_size("tm")
    band, group = lax.axis_index("space"), lax.axis_index("tm")
    line = lambda v: v.reshape(1, channels)
    kernels = conv_weight.reshape(9, 3 * channels, channels)
    gain, bias = line(norm_gain), line(norm_bias)

    def flags(back):
        here = group >= back
        return jnp.stack([here, here & (band > 0), here & (band < bands - 1)]).astype(jnp.int32)[None]

    frame = conv_input
    prev = lax.ppermute(frame, "tm", ring(groups, 1))
    above, below = edges_of(frame)
    total = conv_step(0, flags(0), frame, above, below, gain, bias, kernels, block_input, [line(conv_bias)])
    older = lax.ppermute(prev, "tm", ring(groups, 1))
    above, below = edges_of(prev)
    total = conv_step(1, flags(1), prev, above, below, gain, bias, kernels, total)
    above, below = edges_of(older)
    extra = [line(attn_gain), line(attn_bias), query_weight, line(query_bias), key_weight]
    mixed, normed, queries = conv_step(
        2, flags(2), older, above, below, gain, bias, kernels, total, extra
    )
    closing = [value_weight, line(value_bias), out_weight, line(out_bias), mixed]
    chips = bands // 2
    far = normed
    state = None
    far = [(i, (i + 2) % bands) for i in range(bands)]
    crossing = normed
    waves = []
    for _ in range(chips - 1):
        crossing = lax.ppermute(crossing, "space", far)
        waves.append(crossing)
    near = lax.ppermute(normed, "space", pairs(bands))
    state = attn_step("attn_near", queries, [normed, near], state)
    for i, wave in enumerate(waves):
        beside = lax.ppermute(wave, "space", pairs(bands))
        state = attn_step("attn_far", queries, [wave], state)
        if i < len(waves) - 1:
            state = attn_step("attn_beside", queries, [beside], state)
    result = attn_step("attn_close", queries, [beside], state, closing)
    return result.reshape(block_input.shape)


def from_behind(value, axis, steps):
    count = lax.axis_size(axis)
    leading, last = (max(0, -steps), min(count, count - steps))
    return lax.ppermute(value, axis, [(source, source + steps) for source in range(leading, last)])


def padded_2(x, sides, width):
    for axis, dim in sides:
        peers, length = (lax.axis_size(axis), x.shape[dim])
        up = [(i, (i + 1) % peers) for i in range(peers - 1)]
        down = [(j, i) for i, j in up]
        last = lax.slice_in_dim(x, length - width, length, axis=dim)
        leading = lax.slice_in_dim(x, 0, width, axis=dim)
        before = lax.ppermute(last, axis, up)
        after = lax.ppermute(leading, axis, down)
        x = jnp.concatenate([before, x, after], axis=dim)
    return x


def rms_norm(field, gain, bias):
    mean_square = jnp.mean(field * field, axis=-1, keepdims=True)
    return field * lax.rsqrt(mean_square + 1e-06) * gain + bias


def causal_conv(padded, conv_weight, frame_count, row_count, columns):
    channels = padded.shape[-1]
    running = jnp.zeros((frame_count * row_count * columns, channels), jnp.float32)
    for tap_t in range(3):
        for tap_y in range(3):
            window = padded[tap_t : tap_t + frame_count, tap_y : tap_y + row_count]
            joined = jnp.concatenate(
                [window[:, :, tap_x : tap_x + columns] for tap_x in range(3)], axis=-1
            )
            joined = joined.reshape(-1, 3 * channels)
            kernel = conv_weight[tap_t, tap_y].reshape(3 * channels, channels)
            running = running + jnp.dot(joined, kernel, preferred_element_type=jnp.float32)
    return running.reshape(frame_count, row_count, columns, channels)


def absorb(state, queries, key_rows, value_rows, score_scale):
    numer_acc, denom_acc, max_acc = state
    scores = (
        jnp.einsum("fqc,fkc->fqk", queries, key_rows, preferred_element_type=jnp.float32)
        * score_scale
    )
    new_max = jnp.maximum(max_acc, jnp.max(scores, axis=-1))
    expd = jnp.exp(scores - new_max[..., None])
    weights = expd.astype(jnp.bfloat16)
    added = jnp.einsum("fqk,fkc->fqc", weights, value_rows, preferred_element_type=jnp.float32)
    numer_acc = added
    denom_acc = jnp.sum(expd, axis=-1)
    return (numer_acc, denom_acc, new_max)


def shards(
    block_input,
    conv_input,
    norm_gain,
    norm_bias,
    conv_weight,
    conv_bias,
    attn_gain,
    attn_bias,
    query_weight,
    query_bias,
    key_weight,
    value_weight,
    value_bias,
    out_weight,
    out_bias,
):
    frame_count, row_count, columns, channels = block_input.shape
    if frame_count == 1 and lax.axis_size("space") % 2 == 0 and lax.axis_size("space") > 2:
        return single_frame(
            block_input,
            conv_input,
            norm_gain,
            norm_bias,
            conv_weight,
            conv_bias,
            attn_gain,
            attn_bias,
            query_weight,
            query_bias,
            key_weight,
            value_weight,
            value_bias,
            out_weight,
            out_bias,
        )
    field = conv_input.astype(jnp.float32)
    activated = jax.nn.silu(rms_norm(field, norm_gain, norm_bias)).astype(jnp.bfloat16)
    earlier = [from_behind(activated, "tm", offset) for offset in (1, 2)]
    stacked = jnp.concatenate([earlier[1], earlier[0], activated], axis=0)
    padded = padded_2(stacked, (("space", 1),), 1)
    padded = jnp.pad(padded, ((0, 0), (0, 0), (1, 1), (0, 0)))
    convolved = causal_conv(padded, conv_weight, frame_count, row_count, columns) + conv_bias
    mixed = (block_input.astype(jnp.float32) + convolved).astype(jnp.bfloat16)
    mixed_wide = mixed.astype(jnp.float32)
    normed = rms_norm(mixed_wide, attn_gain, attn_bias).astype(jnp.bfloat16)
    flat_rows = normed.reshape(frame_count, row_count * columns, channels)
    score_scale = float(channels) ** (-0.5)
    queries = (
        jnp.dot(flat_rows, query_weight, preferred_element_type=jnp.float32) + query_bias
    ).astype(jnp.bfloat16)
    query_count = row_count * columns
    start_state = (
        jnp.zeros((frame_count, query_count, channels), jnp.float32),
        jnp.zeros((frame_count, query_count), jnp.float32),
        jnp.full((frame_count, query_count), -1e30, jnp.float32),
    )
    source = lax.all_gather(normed, "space", axis=1, tiled=True).reshape(frame_count, -1, channels)
    key_rows = jnp.dot(source, key_weight, preferred_element_type=jnp.float32).astype(jnp.bfloat16)
    value_rows = (
        jnp.dot(source, value_weight, preferred_element_type=jnp.float32) + value_bias
    ).astype(jnp.bfloat16)
    numer_acc, denom_acc, max_acc = absorb(start_state, queries, key_rows, value_rows, score_scale)
    attended = (numer_acc / denom_acc[..., None]).astype(jnp.bfloat16)
    projected = jnp.dot(attended, out_weight, preferred_element_type=jnp.float32) + out_bias
    return (mixed_wide + projected.reshape(mixed_wide.shape)).astype(jnp.bfloat16)


def solution(mesh):
    placed = (
        P(("clip", "tm"), "space", None, None),
        P(("clip", "tm"), "space", None, None),
        P(),
        P(),
        P(),
        P(),
        P(),
        P(),
        P(),
        P(),
        P(),
        P(),
        P(),
        P(),
        P(),
    )
    return jax.shard_map(
        shards,
        mesh=mesh,
        in_specs=placed,
        out_specs=P(("clip", "tm"), "space", None, None),
        check_vma=False,
    )
```
